32 devices in a mesh: rep: 4 (over y, x), seq: 8 (over z, core).
Axes of the slice: x: 2, y: 2, z: 4, core: 2. Of those that a mesh axis runs over, the one named last changes fastest.
Arguments:
- query: bfloat16 [4096, 2048], P(('rep', 'seq')), parts along dimension 0, may hold values from -6 to 6
- key_proj: bfloat16 [4096, 2048], P(('rep', 'seq')), parts along dimension 0, may hold values from -6 to 6
- value: bfloat16 [4096, 2048], P(('rep', 'seq')), parts along dimension 0, may hold values from -6 to 6
- poles: float32 [2048, 16], replicated, may hold values from 0.00048828125 to 0.05
- residues: float32 [2048, 16], replicated, may hold values from -0.12 to 0.12
- skip: float32 [2048], replicated, may hold values from 0.5 to 2
- w_out: bfloat16 [2048, 4096], P('seq'), may hold values from -0.125 to 0.125
Outputs:
- mixed: bfloat16 [4096, 4096], P(('rep', 'seq')), parts along dimension 0
The draws below stay inside these ranges and needn't reach their ends.
There are 4 independent parts, one for each index of `rep`. The reference program is written for one: setup_inputs(seed, part) draws one part's arguments, and reference() takes and returns one part's arrays. A program takes and returns all parts, laid end to end along the dimension named above; an argument that names none is the same for every part. Nothing has to cross between parts.
All inputs are finite; a program needn't handle non-finite values.
Results may differ from the reference program's by a relative error of at most 0.012.
Values may be sent and summed in bfloat16 or wider, within the bound.
No kernel may reach another device: no remote copies, remote signals or barrier semaphores. Data moves between devices by JAX's collectives and lax.ppermute only.
A program may use at most 128 MiB of HBM per device.

```python
import math
import jax
import jax.numpy as jnp

D = 4096
CH = 2048
ORDER = 16
L = 1024


def level_of(stream_key, shape, shards, low, high):
    def one(dim, blocks):
        heights = jax.random.uniform(jax.random.fold_in(jax.random.fold_in(stream_key, 6), dim), (blocks,), jnp.float32, low / len(shards), high / len(shards))
        return jnp.repeat(jnp.exp(heights), shape[dim] // blocks).reshape((-1,) + (1,) * (len(shape) - dim - 1))

    loudness = one(*shards[0])
    for cut in shards[1:]:
        loudness = loudness * one(*cut)
    return loudness


def gaussian(rng, extent, scale, most, pieces=(), kind=jnp.bfloat16):
    result = jax.random.normal(rng, extent, jnp.float32) * scale
    if len(pieces) > 0:
        result = level_of(rng, extent, pieces, -0.22, 0.18) * result
    return jnp.clip(result, min=-most, max=most).astype(kind)


def setup_inputs(seed: int = 0, part: int = 0) -> dict:
    key_of = jax.random.split(jax.random.key(seed), 8)
    part_splits = jax.random.split(jax.random.fold_in(key_of[7], part), 8)
    return {
        "query": gaussian(part_splits[0], (L, CH), 1.0, 6.0, ((0, 8),)),
        "key_proj": gaussian(part_splits[1], (L, CH), 1.0, 6.0, ((0, 8),)),
        "value": gaussian(part_splits[2], (L, CH), 1.0, 6.0, ((0, 8),)),
        "poles": jnp.clip(jnp.exp(jax.random.uniform(key_of[3], (CH, ORDER), jnp.float32, math.log(0.00048828125), math.log(0.05))), 0.00048828125, 0.05),
        "residues": gaussian(key_of[4], (CH, ORDER), 0.02, 0.12, (), jnp.float32),
        "skip": jnp.clip(jax.random.uniform(key_of[5], (CH,), jnp.float32, 0.5, 2.0), 0.5, 2.0),
        "w_out": gaussian(key_of[6], (CH, D), CH ** -0.5, 0.125, ((0, 8),)),
    }


def reference(query, key_proj, value, poles, residues, skip, w_out):
    product = key_proj.astype(jnp.float32) * value.astype(jnp.float32)
    offsets = jnp.arange(L, dtype=jnp.int32).astype(jnp.float32)[:, None]
    filters = jnp.zeros((L, CH), jnp.float32)
    for order_index in range(ORDER):
        filters = filters + residues[:, order_index][None, :] * jnp.exp(-poles[:, order_index][None, :] * offsets)
    spectrum = jnp.fft.rfft(product, n=2 * L, axis=0) * jnp.fft.rfft(filters, n=2 * L, axis=0)
    convolved = jnp.fft.irfft(spectrum, n=2 * L, axis=0)[:L] + skip[None, :] * product
    gated = (query.astype(jnp.float32) * convolved).astype(jnp.bfloat16)
    return jnp.dot(gated, w_out, preferred_element_type=jnp.float32).astype(jnp.bfloat16)
```

```python
import functools

import jax
import jax.numpy as jnp
from jax import lax
from jax.experimental import pallas as pl
from jax.experimental.pallas import tpu as pltpu
from jax.sharding import PartitionSpec as P

F32 = jnp.float32
BF16 = jnp.bfloat16
LANES = 128
SUBLANES = 8


def permute(array, axis, target):
    size = lax.axis_size(axis)
    return lax.ppermute(array, axis, [(i, target(i)) for i in range(size)])


def swap(array, axis, mask):
    return permute(array, axis, lambda i: i ^ mask)


def fill_product(key_ref, value_ref, prod_ref):
    tokens, channels = key_ref.shape
    for tile in range(channels // LANES):
        cols = slice(tile * LANES, (tile + 1) * LANES)
        prod_ref[tile * tokens : (tile + 1) * tokens, :] = key_ref[:, cols].astype(F32) * value_ref[:, cols].astype(F32)


def state_kernel(key_ref, value_ref, poles_ref, state_ref, prod_ref):
    tokens = key_ref.shape[0]
    order, tiles, _ = poles_ref.shape
    fill_product(key_ref, value_ref, prod_ref)
    for first in range(0, tiles, SUBLANES):
        group = slice(first, first + SUBLANES)
        decay = [jnp.exp(-poles_ref[r, group, :]) for r in range(order)]

        def step(t, state):
            x = prod_ref[pl.ds(first * tokens + t, SUBLANES, stride=tokens), :]
            return tuple(decay[r] * state[r] + x for r in range(order))

        zero = jnp.zeros((SUBLANES, LANES), F32)
        state = lax.fori_loop(0, tokens, step, (zero,) * order, unroll=4)
        for r in range(order):
            state_ref[r, group, :] = state[r]


def convolve_kernel(query_ref, key_ref, value_ref, poles_ref, residues_ref, skip_ref, carry_ref, gated_ref, prod_ref):
    tokens, channels = key_ref.shape
    order, tiles, _ = poles_ref.shape
    fill_product(key_ref, value_ref, prod_ref)
    for first in range(0, tiles, SUBLANES):
        group = slice(first, first + SUBLANES)
        decay = [jnp.exp(-poles_ref[r, group, :]) for r in range(order)]
        skip = skip_ref[group, :]

        def step(t, state):
            rows = pl.ds(first * tokens + t, SUBLANES, stride=tokens)
            x = prod_ref[rows, :]
            state = tuple(decay[r] * state[r] + x for r in range(order))
            parts = [residues_ref[r, group, :] * state[r] for r in range(order)] + [skip * x]
            while len(parts) > 1:
                parts = [sum(parts[i : i + 2][1:], parts[i]) for i in range(0, len(parts), 2)]
            prod_ref[rows, :] = parts[0]
            return state

        lax.fori_loop(0, tokens, step, tuple(carry_ref[r, group, :] for r in range(order)), unroll=4)
    for tile in range(channels // LANES):
        cols = slice(tile * LANES, (tile + 1) * LANES)
        y = prod_ref[tile * tokens : (tile + 1) * tokens, :]
        gated_ref[:, cols] = (query_ref[:, cols].astype(F32) * y).astype(BF16)


def project_kernel(pieces, blocks, index_ref, *refs):
    gated, weights, outs, total = (
        refs[:pieces],
        refs[pieces : pieces + blocks],
        refs[pieces + blocks : 2 * pieces + blocks],
        refs[-1],
    )
    tokens = gated[0].shape[0]
    for b in range(blocks):
        depth = weights[b].shape[0]
        start = pl.multiple_of(index_ref[b] * depth, depth)
        left = jnp.concatenate([g[:, pl.ds(start, depth)] for g in gated], axis=0)
        part = jnp.dot(left, weights[b][...], preferred_element_type=F32)
        if b == 0:
            total[...] = part
        else:
            total[...] += part
    for i in range(pieces):
        outs[i][...] = total[i * tokens : (i + 1) * tokens, :].astype(BF16)


def place_kernel(index_ref, *refs):
    out_ref = refs[-1]
    for i, piece in enumerate(refs[:-1]):
        width = piece.shape[1]
        start = pl.multiple_of(index_ref[i] * width, width)
        out_ref[:, pl.ds(start, width)] = piece[...]


def whole(count, space=pltpu.VMEM):
    return [pl.BlockSpec(memory_space=space)] * count


def call(kernel, name, out_shapes, args, scratch=(), scalars=0, flops=0):
    out_shapes = [jax.ShapeDtypeStruct(s, d) for s, d in out_shapes]
    moved = sum(a.size * a.dtype.itemsize for a in list(args) + out_shapes)
    return pl.pallas_call(
        kernel,
        name=name,
        out_shape=out_shapes,
        in_specs=whole(scalars, pltpu.SMEM) + whole(len(args) - scalars),
        out_specs=whole(len(out_shapes)),
        scratch_shapes=list(scratch),
        cost_estimate=pl.CostEstimate(flops=flops, bytes_accessed=moved, transcendentals=0),
    )(*args)


def carry_in(state, poles, tokens, members):
    seq = lax.axis_index("seq")
    half = state.shape[1] // 2

    def decay(count, rates):
        return jnp.exp(-rates * float(count * tokens))

    core = seq % 2
    other = swap(state, "seq", 1)
    first = core == 0
    rate = decay(1, poles)
    both = rate * jnp.where(first, state, other) + jnp.where(first, other, state)
    start = core * half
    mine = lax.dynamic_slice_in_dim(both, start, half, 1)
    my_poles = lax.dynamic_slice_in_dim(poles, start, half, 1)
    prefix = jnp.zeros_like(mine)
    total = mine
    span = 2
    while span < members:
        arrived = swap(total, "seq", span)
        upper = (seq // span) % 2 == 1
        ahead = (seq % span) // 2 * 2
        scale = jnp.exp(-my_poles * (ahead * tokens).astype(F32))
        prefix = prefix + jnp.where(upper, scale * arrived, 0.0)
        if span * 2 < members:
            step = decay(span, my_poles)
            total = step * jnp.where(upper, arrived, total) + jnp.where(upper, total, arrived)
        span *= 2
    rest = swap(prefix, "seq", 1)
    carry = jnp.where(first, jnp.concatenate([prefix, rest], 1), jnp.concatenate([rest, prefix], 1))
    return jnp.where(first, carry, rate * carry + other)


def gather_rows(block, members):
    seq = lax.axis_index("seq")
    if members != 8:
        rows = lax.all_gather(block, "seq", axis=0, tiled=True)
        return [rows], jnp.zeros((1,), jnp.int32)
    spot = seq // 2
    inner = (spot == 1) | (spot == 2)

    def middle(i):
        return {2: 4, 3: 5, 4: 2, 5: 3}.get(i, i ^ 1)

    near = swap(block, "seq", 2)
    across = permute(block, "seq", middle)
    near_next = swap(across, "seq", 2)
    across_next = permute(near, "seq", middle)
    far = swap(across_next, "seq", 2)
    second = jnp.where(inner, across, near_next)
    third = jnp.where(inner, across_next, far)
    mine = [block, near, second, third]
    theirs = [swap(b, "seq", 1) for b in mine]
    core = seq % 2
    spots = [spot, spot ^ 1, jnp.where(inner, 3 - spot, spot ^ 2), jnp.where(inner, spot ^ 2, 3 - spot)]
    places = [p * 2 + core for p in spots] + [p * 2 + 1 - core for p in spots]
    return mine + theirs, jnp.stack(places).astype(jnp.int32)


def shards(query, key_proj, value, poles, residues, skip, w_out):
    tokens, channels = query.shape
    width = w_out.shape[1]
    members = lax.axis_size("seq")
    parts = lax.axis_size("rep")
    order = poles.shape[1]
    tiles = channels // LANES
    rep = lax.axis_index("rep")
    columns = width // parts

    block = lax.dynamic_slice_in_dim(w_out, rep * columns, columns, 1)
    weights, places = gather_rows(block, members)

    poles = poles.T.reshape(order, tiles, LANES)
    residues = residues.T.reshape(order, tiles, LANES)
    skip = skip.reshape(tiles, LANES)
    scratch = [pltpu.VMEM((tiles * tokens, LANES), F32)]
    work = tokens * channels * order
    (state,) = call(
        state_kernel, "states", [((order, tiles, LANES), F32)], (key_proj, value, poles), scratch, flops=2 * work
    )
    carry = carry_in(state, poles, tokens, members)
    (gated,) = call(
        convolve_kernel,
        "convolve",
        [((tokens, channels), BF16)],
        (query, key_proj, value, poles, residues, skip, carry),
        scratch,
        flops=4 * work,
    )
    gathered = [gated] + [swap(gated, "rep", i) for i in range(1, parts)]
    blocks = call(
        functools.partial(project_kernel, parts, len(weights)),
        "project",
        [((tokens, columns), BF16)] * parts,
        (places, *gathered, *weights),
        [pltpu.VMEM((parts * tokens, columns), F32)],
        scalars=1,
        flops=2 * parts * tokens * channels * columns,
    )
    pieces = [blocks[0]] + [swap(blocks[i], "rep", i) for i in range(1, parts)]
    order_of = (rep ^ jnp.arange(parts, dtype=jnp.int32)).astype(jnp.int32)
    (mixed,) = call(place_kernel, "place", [((tokens, width), BF16)], (order_of, *pieces), scalars=1)
    return mixed


def solution(mesh):
    return jax.shard_map(
        shards,
        mesh=mesh,
        in_specs=(
            P(("rep", "seq"), None),
            P(("rep", "seq"), None),
            P(("rep", "seq"), None),
            P(),
            P(),
            P(),
            P("seq", None),
        ),
        out_specs=P(("rep", "seq"), None),
        check_vma=False,
    )
```

```python
import functools
import math

import jax
import jax.numpy as jnp
from jax import lax
from jax.experimental import pallas as pl
from jax.experimental.pallas import tpu as pltpu
from jax.sharding import PartitionSpec as P


F32 = jnp.float32
BF16 = jnp.bfloat16
LANES = 128
SUBLANES = 8


def permute(array, axis, target):
    size = lax.axis_size(axis)
    return lax.ppermute(array, axis, [(i, target(i)) for i in range(size)])


def swap(array, axis, mask):
    return permute(array, axis, lambda i: i ^ mask)


def fill_product(key_ref, value_ref, prod_ref):
    tokens, channels = key_ref.shape
    for tile in range(channels // LANES):
        cols = slice(tile * LANES, (tile + 1) * LANES)
        prod_ref[tile * tokens : (tile + 1) * tokens, :] = key_ref[:, cols].astype(F32) * value_ref[:, cols].astype(F32)


def group_of(core_ref, slot, tiles):
    half = tiles // 2
    side = core_ref[0] if slot == 0 else 1 - core_ref[0]
    return pl.multiple_of(side * half, SUBLANES), half


def state_kernel(core_ref, key_ref, value_ref, poles_ref, kept_ref, sent_ref, rate_ref, prod_ref):
    tokens = key_ref.shape[0]
    order, tiles, _ = poles_ref.shape
    fill_product(key_ref, value_ref, prod_ref)
    for slot, state_ref in ((1, sent_ref), (0, kept_ref)):
        start, half = group_of(core_ref, slot, tiles)
        for row in range(0, half, SUBLANES):
            first = pl.multiple_of(start + row, SUBLANES)
            poles = [poles_ref[r, pl.ds(first, SUBLANES), :] for r in range(order)]
            decay = [jnp.exp(-p) for p in poles]

            def step(t, state):
                x = prod_ref[pl.ds(first * tokens + t, SUBLANES, stride=tokens), :]
                return tuple(decay[r] * state[r] + x for r in range(order))

            zero = jnp.zeros((SUBLANES, LANES), F32)
            state = lax.fori_loop(0, tokens, step, (zero,) * order, unroll=8)
            for r in range(order):
                state_ref[r, row : row + SUBLANES, :] = state[r]
                if slot == 0:
                    rate_ref[r, row : row + SUBLANES, :] = jnp.exp(-poles[r] * float(tokens))


def local_kernel(key_ref, value_ref, poles_ref, residues_ref, skip_ref, local_ref):
    tokens = key_ref.shape[0]
    order, tiles, _ = poles_ref.shape
    fill_product(key_ref, value_ref, local_ref)
    for first in range(0, tiles, SUBLANES):
        group = slice(first, first + SUBLANES)
        decay = [jnp.exp(-poles_ref[r, group, :]) for r in range(order)]
        skip = skip_ref[group, :]

        def step(t, state):
            rows = pl.ds(first * tokens + t, SUBLANES, stride=tokens)
            x = local_ref[rows, :]
            state = tuple(decay[r] * state[r] + x for r in range(order))
            parts = [residues_ref[r, group, :] * state[r] for r in range(order)] + [skip * x]
            local_ref[rows, :] = tree_sum(parts)
            return state

        zero = jnp.zeros((SUBLANES, LANES), F32)
        lax.fori_loop(0, tokens, step, (zero,) * order, unroll=4)


def tree_sum(parts):
    while len(parts) > 1:
        parts = [parts[i] if i + 1 == len(parts) else parts[i] + parts[i + 1] for i in range(0, len(parts), 2)]
    return parts[0]


def carry_kernel(core_ref, query_ref, local_ref, poles_ref, residues_ref, kept_ref, sent_ref, *refs):
    gated_refs, total_ref, starts_ref = refs[:-2], refs[-2], refs[-1]
    tokens, channels = query_ref.shape
    order, tiles, _ = poles_ref.shape
    stretch = 16 if tokens % 16 == 0 else tokens
    for slot, carry_ref in ((0, kept_ref), (1, sent_ref)):
        start, half = group_of(core_ref, slot, tiles)
        for row in range(0, half, SUBLANES):
            first = pl.multiple_of(start + row, SUBLANES)
            group = pl.ds(first, SUBLANES)
            jump = [jnp.exp(-poles_ref[r, group, :] * float(stretch)) for r in range(order)]
            state = [carry_ref[r, row : row + SUBLANES, :] for r in range(order)]
            for i in range(tokens // stretch):
                for r in range(order):
                    starts_ref[i, r] = state[r]
                state = [jump[r] * state[r] for r in range(order)]
            decay = [jnp.exp(-poles_ref[r, group, :]) for r in range(order)]

            def step(j, weight):
                weight = tuple(decay[r] * weight[r] for r in range(order))
                for i in range(tokens // stretch):
                    rows = pl.ds(first * tokens + i * stretch + j, SUBLANES, stride=tokens)
                    parts = [weight[r] * starts_ref[i, r] for r in range(order)] + [local_ref[rows, :]]
                    total_ref[rows, :] = tree_sum(parts)
                return weight

            lax.fori_loop(0, stretch, step, tuple(residues_ref[r, group, :] for r in range(order)))
    step_rows = tokens // len(gated_refs)
    for tile in range(channels // LANES):
        cols = slice(tile * LANES, (tile + 1) * LANES)
        y = total_ref[tile * tokens : (tile + 1) * tokens, :]
        gated = (query_ref[:, cols].astype(F32) * y).astype(BF16)
        for i, ref in enumerate(gated_refs):
            ref[:, cols] = gated[i * step_rows : (i + 1) * step_rows, :]


def project_kernel(pieces, blocks, chunks, index_ref, *refs):
    gated, weights = refs[:pieces], [refs[pieces + n * blocks : pieces + (n + 1) * blocks] for n in range(chunks)]
    outs, (left, right, left_sem, right_sem) = refs[pieces + chunks * blocks : -4], refs[-4:]
    tokens = gated[0].shape[0]
    depth, columns = weights[0][0].shape
    copies = []
    for n in range(chunks):
        for b in range(blocks):
            start = pl.multiple_of(index_ref[b] * depth, depth)
            place = right.at[pl.ds(start, depth), pl.ds(n * columns, columns)]
            copies.append(pltpu.make_async_copy(weights[n][b], place, right_sem.at[n * blocks + b]))
    for i in range(pieces):
        copies.append(pltpu.make_async_copy(gated[i], left.at[pl.ds(i * tokens, tokens), :], left_sem.at[i]))
    for copy in copies:
        copy.start()
    for copy in copies:
        copy.wait()
    total = jnp.dot(left[...], right[...], preferred_element_type=F32).astype(BF16)
    rows = total.shape[0] // len(outs)
    for i, out in enumerate(outs):
        out[...] = total[i * rows : (i + 1) * rows, :]


def place_kernel(aliased, index_ref, *refs):
    pieces, (out_ref, held, in_sem, out_sem) = refs[:-4], refs[-4:]
    if aliased:
        pieces = pieces[1:]
    arrive = [pltpu.make_async_copy(piece, held.at[i], in_sem.at[i]) for i, piece in enumerate(pieces)]
    for copy in arrive:
        copy.start()
    leave = []
    for i, piece in enumerate(pieces):
        width = piece.shape[1]
        start = pl.multiple_of(index_ref[i] * width, width)
        leave.append(pltpu.make_async_copy(held.at[i], out_ref.at[:, pl.ds(start, width)], out_sem.at[i]))
    for i in range(len(pieces)):
        arrive[i].wait()
        leave[i].start()
    for copy in leave:
        copy.wait()


def whole(count, space=pltpu.VMEM):
    return [pl.BlockSpec(memory_space=space)] * count


def call(kernel, out_shapes, args, scratch=(), scalars=0, flops=0, inputs=pltpu.VMEM, outputs=pltpu.VMEM, aliases=None):
    out_shapes = [jax.ShapeDtypeStruct(s, d) for s, d in out_shapes]
    moved = sum(a.size * a.dtype.itemsize for a in list(args) + out_shapes)
    held = sum(math.prod(m.shape) * jnp.dtype(m.dtype).itemsize for m in scratch if m.memory_space == pltpu.VMEM)
    held += moved if inputs == pltpu.VMEM else 0
    return pl.pallas_call(
        kernel,
        out_shape=out_shapes,
        in_specs=whole(scalars, pltpu.SMEM) + whole(len(args) - scalars, inputs),
        out_specs=whole(len(out_shapes), outputs),
        scratch_shapes=list(scratch),
        input_output_aliases=aliases or {},
        compiler_params=pltpu.CompilerParams(vmem_limit_bytes=min(2 * held + (4 << 20), 60 << 20)),
        cost_estimate=pl.CostEstimate(flops=flops, bytes_accessed=moved, transcendentals=0),
    )(*args)


def carry_in(kept, sent, rate, members):
    seq = lax.axis_index("seq")
    first = seq % 2 == 0
    other = swap(sent, "seq", 1)
    early = jnp.where(first, kept, other)
    total = rate * early + jnp.where(first, other, kept)
    prefix = jnp.zeros_like(total)
    ahead = jnp.ones_like(total)
    step = rate * rate
    span = 2
    while span < members:
        arrived = swap(total, "seq", span)
        upper = (seq // span) % 2 == 1
        prefix = prefix + jnp.where(upper, ahead * arrived, 0.0)
        ahead = jnp.where(upper, ahead * step, ahead)
        total = step * jnp.where(upper, arrived, total) + jnp.where(upper, total, arrived)
        step = step * step
        span *= 2
    later = rate * prefix + early
    rest = swap(jnp.where(first, later, prefix), "seq", 1)
    return jnp.where(first, prefix, later), rest


def gather_rows(block, members):
    seq = lax.axis_index("seq")
    if members != 8:
        rows = lax.all_gather(block, "seq", axis=0, tiled=True)
        return [rows], jnp.zeros((1,), jnp.int32)
    spot = seq // 2
    inner = (spot == 1) | (spot == 2)

    def middle(i):
        return {2: 4, 3: 5, 4: 2, 5: 3}.get(i, i ^ 1)

    near = swap(block, "seq", 2)
    across = permute(block, "seq", middle)
    near_next = swap(across, "seq", 2)
    across_next = permute(near, "seq", middle)
    far = swap(across_next, "seq", 2)
    second = jnp.where(inner, across, near_next)
    third = jnp.where(inner, across_next, far)
    mine = [block, near, second, third]
    theirs = [swap(b, "seq", 1) for b in mine]
    core = seq % 2
    spots = [spot, spot ^ 1, jnp.where(inner, 3 - spot, spot ^ 2), jnp.where(inner, spot ^ 2, 3 - spot)]
    places = [p * 2 + core for p in spots] + [p * 2 + 1 - core for p in spots]
    return mine + theirs, jnp.stack(places).astype(jnp.int32)


def gather_parts(halves, parts):
    if parts != 4 or len(halves) != 2:
        return [halves] + [[swap(h, "rep", i) for h in halves] for i in range(1, parts)]
    one = [swap(h, "rep", 1) for h in halves]
    two = [swap(h, "rep", 2) for h in halves]
    three = [swap(two[0], "rep", 1), swap(one[1], "rep", 2)]
    return [halves, one, two, three]


def shards(chunks, query, key_proj, value, poles, residues, skip, w_out):
    tokens, channels = query.shape
    width = w_out.shape[1]
    members = lax.axis_size("seq")
    parts = lax.axis_size("rep")
    order = poles.shape[1]
    tiles = channels // LANES
    rep = lax.axis_index("rep")
    part_width = width // parts
    columns = part_width // chunks

    weights = []
    for n in range(chunks):
        block = lax.dynamic_slice_in_dim(w_out, (rep * chunks + n) * columns, columns, 1)
        rows, places = gather_rows(block, members)
        weights.append(rows)

    poles = poles.T.reshape(order, tiles, LANES)
    residues = residues.T.reshape(order, tiles, LANES)
    skip = skip.reshape(tiles, LANES)
    core = (lax.axis_index("seq") % 2).astype(jnp.int32).reshape(1)
    sums = pltpu.VMEM((tiles * tokens, LANES), F32)
    work = tokens * channels * order
    state_shape = ((order, tiles // 2, LANES), F32)
    kept, sent, rate = call(
        state_kernel, [state_shape] * 3, (core, key_proj, value, poles), [sums], scalars=1, flops=2 * work
    )
    kept, sent = carry_in(kept, sent, rate, members)
    (local,) = call(
        local_kernel, [((tiles * tokens, LANES), F32)], (key_proj, value, poles, residues, skip), flops=4 * work
    )
    halves = call(
        carry_kernel,
        [((tokens // 2, channels), BF16)] * 2,
        (core, query, local, poles, residues, kept, sent),
        [sums, pltpu.VMEM((tokens // 16, order, SUBLANES, LANES), F32)],
        scalars=1,
        flops=2 * work,
    )
    gathered = gather_parts(list(halves), parts)
    count = len(weights[0])
    blocks = []
    for group in (gathered[:-1], gathered[-1:]):
        held = sum(group, [])
        blocks += call(
            functools.partial(project_kernel, len(held), count, chunks),
            [((tokens, part_width), BF16)] * len(group),
            (places, *held, *sum(weights, [])),
            [
                pltpu.VMEM((len(group) * tokens, channels), BF16),
                pltpu.VMEM((channels, part_width), BF16),
                pltpu.SemaphoreType.DMA((len(held),)),
                pltpu.SemaphoreType.DMA((chunks * count,)),
            ],
            scalars=1,
            flops=2 * len(group) * tokens * channels * part_width,
            inputs=pl.ANY,
        )
    pieces = [blocks[0]] + [swap(blocks[i], "rep", i) for i in range(1, parts)]
    spots = (rep ^ jnp.arange(parts, dtype=jnp.int32)).astype(jnp.int32)
    mixed = None
    for group in (range(parts - 1), range(parts - 1, parts)):
        first = mixed is None
        (mixed,) = call(
            functools.partial(place_kernel, not first),
            [((tokens, width), BF16)],
            (spots[group[0] :], *([] if first else [mixed]), *[pieces[i] for i in group]),
            [
                pltpu.VMEM((len(group), tokens, part_width), BF16),
                pltpu.SemaphoreType.DMA((len(group),)),
                pltpu.SemaphoreType.DMA((len(group),)),
            ],
            scalars=1,
            inputs=pl.ANY,
            outputs=pl.ANY,
            aliases=None if first else {1: 0},
        )
    return mixed


def solution(mesh):
    chunks = 2

    def body(*args):
        return shards(chunks, *args)

    return jax.shard_map(
        body,
        mesh=mesh,
        in_specs=(
            P(("rep", "seq"), None),
            P(("rep", "seq"), None),
            P(("rep", "seq"), None),
            P(),
            P(),
            P(),
            P("seq", None),
        ),
        out_specs=P(("rep", "seq"), None),
        check_vma=False,
    )
```

```python
import functools
import math

import jax
import jax.numpy as jnp
from jax import lax
from jax.experimental import pallas as pl
from jax.experimental.pallas import tpu as pltpu
from jax.sharding import PartitionSpec as P


F32 = jnp.float32
BF16 = jnp.bfloat16
LANES = 128
SUBLANES = 8


def permute(array, axis, target):
    size = lax.axis_size(axis)
    return lax.ppermute(array, axis, [(i, target(i)) for i in range(size)])


def swap(array, axis, mask):
    return permute(array, axis, lambda i: i ^ mask)


def position(axis):
    return lax.axis_index(axis).astype(jnp.int32)


def spread(ref, out_ref):
    order = ref.shape[0]
    for tile in range(ref.shape[1] // LANES):
        out_ref[tile * order : (tile + 1) * order, :] = ref[:, tile * LANES : (tile + 1) * LANES]


def modes_of(ref, first, order):
    return [ref[pl.ds(first * order + r, SUBLANES, stride=order), :] for r in range(order)]


def tree_sum(parts):
    while len(parts) > 1:
        parts = [parts[i] if i + 1 == len(parts) else parts[i] + parts[i + 1] for i in range(0, len(parts), 2)]
    return parts[0]


def group_of(slot, tiles):
    half = tiles // 2
    core = position("seq") & 1
    side = core if slot == 0 else 1 - core
    return pl.multiple_of(side * half, SUBLANES), half


def multiply(key_ref, value_ref, prod_ref):
    tokens, channels = key_ref.shape
    for tile in range(channels // LANES):
        cols = slice(tile * LANES, (tile + 1) * LANES)
        prod_ref[tile * tokens : (tile + 1) * tokens, :] = key_ref[:, cols].astype(F32) * value_ref[:, cols].astype(F32)


def slice_kernel(rows_ref, *refs):
    outs, sems = refs[:-1], refs[-1]
    columns = outs[0].shape[1]
    copies = []
    for i, out in enumerate(outs):
        start = pl.multiple_of((position("rep") * len(outs) + i) * columns, columns)
        copies.append(pltpu.make_async_copy(rows_ref.at[:, pl.ds(start, columns)], out, sems.at[i]))
    for copy in copies:
        copy.start()
    for copy in copies:
        copy.wait()


def state_kernel(*refs):
    fetched, (kept_ref, sent_ref, rate_ref) = refs[:3], refs[3:6]
    key_ref, value_ref, poles_ref, prod_ref, modes_ref, sems = refs[6:]
    copies = [
        pltpu.make_async_copy(source, held, sems.at[i])
        for i, (source, held) in enumerate(zip(fetched, (key_ref, value_ref, poles_ref)))
    ]
    for copy in copies:
        copy.start()
    for copy in copies:
        copy.wait()
    tokens, channels = key_ref.shape
    order, tiles = poles_ref.shape[0], channels // LANES
    spread(poles_ref, modes_ref)
    multiply(key_ref, value_ref, prod_ref)
    for slot, state_ref in ((1, sent_ref), (0, kept_ref)):
        start, half = group_of(slot, tiles)
        for row in range(0, half, SUBLANES):
            first = pl.multiple_of(start + row, SUBLANES)
            poles = modes_of(modes_ref, first, order)
            decay = [jnp.exp(-p) for p in poles]

            def step(t, state):
                x = prod_ref[pl.ds(first * tokens + t, SUBLANES, stride=tokens), :]
                return tuple(decay[r] * state[r] + x for r in range(order))

            zero = jnp.zeros((SUBLANES, LANES), F32)
            state = lax.fori_loop(0, tokens, step, (zero,) * order, unroll=8)
            for r in range(order):
                state_ref[r, row : row + SUBLANES, :] = state[r]
                if slot == 0:
                    rate_ref[r, row : row + SUBLANES, :] = jnp.exp(-poles[r] * float(tokens))


def local_kernel(key_ref, value_ref, poles_ref, residues_ref, skip_ref, local_ref, modes_ref, gains_ref, packed_ref):
    order, channels = poles_ref.shape
    tiles = channels // LANES
    tokens = key_ref.shape[0]
    spread(poles_ref, modes_ref)
    spread(residues_ref, gains_ref)
    multiply(key_ref, value_ref, local_ref)
    for first in range(0, tiles, SUBLANES):
        decay = [jnp.exp(-p) for p in modes_of(modes_ref, first, order)]
        for r, gain in enumerate(modes_of(gains_ref, first, order)):
            packed_ref[r] = gain
        skip = skip_ref[first : first + SUBLANES, :]

        def step(t, state):
            rows = pl.ds(first * tokens + t, SUBLANES, stride=tokens)
            x = local_ref[rows, :]
            state = tuple(decay[r] * state[r] + x for r in range(order))
            local_ref[rows, :] = tree_sum([packed_ref[r] * state[r] for r in range(order)] + [skip * x])
            return state

        zero = jnp.zeros((SUBLANES, LANES), F32)
        lax.fori_loop(0, tokens, step, (zero,) * order, unroll=4)


def carry_kernel(span, query_ref, local_ref, poles_ref, residues_ref, *refs):
    states, gated_refs = (refs[0:2], refs[2:4]), refs[4:-6]
    total_ref, starts_ref, modes_ref, gains_ref, held_ref, sem = refs[-6:]
    fetch = pltpu.make_async_copy(query_ref, held_ref, sem)
    fetch.start()
    tokens, channels = query_ref.shape
    order, tiles = poles_ref.shape[0], channels // LANES
    stretch = 16 if tokens % 16 == 0 else tokens
    spread(poles_ref, modes_ref)
    spread(residues_ref, gains_ref)
    shape = (SUBLANES, LANES)
    seq = position("seq")
    distance = jnp.full(shape, (seq & (span - 1)) * tokens, jnp.int32).astype(F32)
    counts = jnp.full(shape, (seq & span) != 0)
    for slot, (base_ref, arrived_ref) in enumerate(states):
        start, half = group_of(slot, tiles)
        for row in range(0, half, SUBLANES):
            first = pl.multiple_of(start + row, SUBLANES)
            poles = modes_of(modes_ref, first, order)
            jump = [jnp.exp(-p * float(stretch)) for p in poles]
            state = []
            for r in range(order):
                rows = slice(row, row + SUBLANES)
                reach = jnp.exp(-poles[r] * distance) * arrived_ref[r, rows, :]
                state.append(base_ref[r, rows, :] + jnp.where(counts, reach, 0.0))
            for i in range(tokens // stretch):
                for r in range(order):
                    starts_ref[i, r] = state[r]
                state = [jump[r] * state[r] for r in range(order)]
            decay = [jnp.exp(-p) for p in poles]

            def step(j, weight):
                weight = tuple(decay[r] * weight[r] for r in range(order))
                for i in range(tokens // stretch):
                    rows = pl.ds(first * tokens + i * stretch + j, SUBLANES, stride=tokens)
                    parts = [weight[r] * starts_ref[i, r] for r in range(order)] + [local_ref[rows, :]]
                    total_ref[rows, :] = tree_sum(parts)
                return weight

            lax.fori_loop(0, stretch, step, tuple(modes_of(gains_ref, first, order)))
    fetch.wait()
    step_rows = tokens // len(gated_refs)
    for tile in range(tiles):
        cols = slice(tile * LANES, (tile + 1) * LANES)
        y = total_ref[tile * tokens : (tile + 1) * tokens, :]
        gated = (held_ref[:, cols].astype(F32) * y).astype(BF16)
        for i, ref in enumerate(gated_refs):
            ref[:, cols] = gated[i * step_rows : (i + 1) * step_rows, :]


def project_kernel(pieces, places_of, chunks, earlier, *refs):
    places = places_of(position("seq"))
    blocks = len(places)
    gated, refs = refs[:pieces], refs[pieces:]
    weights, refs = refs[: blocks * chunks], refs[blocks * chunks :]
    before, outs = (refs[:chunks], refs[chunks:]) if earlier else (None, refs)
    depth, columns = weights[0].shape
    group = 2 if blocks % 2 == 0 else 1
    for n in range(chunks):
        total = before[n][...] if earlier else None
        for b in range(0, blocks, group):
            starts = [pl.multiple_of(places[b + i] * depth, depth) for i in range(group)]
            left = jnp.concatenate(
                [jnp.concatenate([g[:, pl.ds(s, depth)] for s in starts], axis=1) for g in gated], axis=0
            )
            right = jnp.concatenate([weights[n * blocks + b + i][...] for i in range(group)], axis=0)
            part = jnp.dot(left, right, preferred_element_type=F32)
            total = part if total is None else total + part
        if outs[0].dtype == F32:
            outs[n][...] = total
        else:
            rows = total.shape[0] // len(outs)
            for i, out in enumerate(outs):
                out[:, n * columns : (n + 1) * columns] = total[i * rows : (i + 1) * rows, :].astype(BF16)


def place_kernel(group, aliased, *refs):
    pieces, (out_ref, sems) = refs[int(aliased) : -2], refs[-2:]
    copies = []
    for i, piece in enumerate(pieces):
        width = piece.shape[1]
        start = pl.multiple_of((position("rep") ^ group[i]) * width, width)
        copies.append(pltpu.make_async_copy(piece, out_ref.at[:, pl.ds(start, width)], sems.at[i]))
    for copy in copies:
        copy.start()
    for copy in copies:
        copy.wait()


def call(kernel, out_shapes, args, scratch=(), flops=0, inputs=None, outputs=pltpu.VMEM, aliases=None):
    out_shapes = [jax.ShapeDtypeStruct(s, d) for s, d in out_shapes]
    inputs = inputs or [pltpu.VMEM] * len(args)
    size = lambda a: math.prod(a.shape) * jnp.dtype(a.dtype).itemsize
    held = sum(size(a) for a, space in zip(args, inputs) if space == pltpu.VMEM)
    held += sum(size(a) for a in out_shapes if outputs == pltpu.VMEM)
    held += sum(size(m) for m in scratch if getattr(m, "memory_space", None) == pltpu.VMEM)
    return pl.pallas_call(
        kernel,
        out_shape=out_shapes,
        in_specs=[pl.BlockSpec(memory_space=space) for space in inputs],
        out_specs=[pl.BlockSpec(memory_space=outputs)] * len(out_shapes),
        scratch_shapes=list(scratch),
        input_output_aliases=aliases or {},
        compiler_params=pltpu.CompilerParams(vmem_limit_bytes=min(2 * held + (2 << 20), 60 << 20)),
        cost_estimate=pl.CostEstimate(
            flops=flops, bytes_accessed=sum(size(a) for a in list(args) + out_shapes), transcendentals=0
        ),
    )(*args)


def fused(function, args, count):
    def kernel(*refs):
        for i in range(refs[0].shape[0]):
            results = function(*[ref[i] for ref in refs[: len(args)]])
            for ref, result in zip(refs[len(args) :], results):
                ref[i] = result

    return call(kernel, [(args[0].shape, args[0].dtype)] * count, args)


def carry_in(kept, sent, rate, members):
    def bit(span):
        return (position("seq") & span) != 0

    other = swap(sent, "seq", 1)

    def pair(rate, kept, other):
        later = bit(1)
        return (rate * jnp.where(later, other, kept) + jnp.where(later, kept, other),)

    (total,) = fused(pair, (rate, kept, other), 1)
    span = 2
    carried = ()
    while span * 2 < members:
        arrived = swap(total, "seq", span)

        def join(rate, total, arrived, *carried, span=span):
            prefix, ahead = carried or (jnp.zeros_like(rate), jnp.ones_like(rate))
            step = rate
            for _ in range(span.bit_length() - 1):
                step = step * step
            upper = bit(span)
            prefix = prefix + jnp.where(upper, ahead * arrived, 0.0)
            ahead = jnp.where(upper, ahead * step, ahead)
            total = step * jnp.where(upper, arrived, total) + jnp.where(upper, total, arrived)
            return total, prefix, ahead

        total, *carried = fused(join, (rate, total, arrived, *carried), 3)
        span *= 2
    arrived = swap(total, "seq", span)

    def bases(rate, kept, other, prefix):
        second = bit(1)
        early = jnp.where(second, other, kept)
        later = rate * prefix + early
        return jnp.where(second, later, prefix), jnp.where(second, prefix, later)

    own, away = fused(bases, (rate, kept, other, carried[0]), 2)
    rest = swap(away, "seq", 1)
    return own, arrived, rest, swap(arrived, "seq", 1), span


def gather_rows(block, members):
    if members != 8:
        rows = lax.all_gather(block, "seq", axis=0, tiled=True)
        return [rows], lambda seq: [0]

    def inner(seq):
        spot = seq >> 1
        return (spot == 1) | (spot == 2)

    def choose(first, second):
        def kernel(first_ref, second_ref, out_ref):
            @pl.when(inner(position("seq")))
            def _():
                out_ref[...] = first_ref[...]

            @pl.when(jnp.logical_not(inner(position("seq"))))
            def _():
                out_ref[...] = second_ref[...]

        return call(kernel, [(first.shape, first.dtype)], (first, second))[0]

    def middle(i):
        return {2: 4, 3: 5, 4: 2, 5: 3}.get(i, i ^ 1)

    near = swap(block, "seq", 2)
    across = permute(block, "seq", middle)
    near_next = swap(across, "seq", 2)
    across_next = permute(near, "seq", middle)
    far = swap(across_next, "seq", 2)
    second = choose(across, near_next)
    third = choose(across_next, far)
    mine = [block, near, second, third]
    theirs = [swap(b, "seq", 1) for b in mine]

    def places(seq):
        spot, core = seq >> 1, seq & 1
        opposite, skipped = 3 - spot, spot ^ 2
        spots = [
            spot,
            spot ^ 1,
            jnp.where(inner(seq), opposite, skipped),
            jnp.where(inner(seq), skipped, opposite),
        ]
        return sum(([p * 2 + core, p * 2 + 1 - core] for p in spots), [])

    return sum(([m, t] for m, t in zip(mine, theirs)), []), places


def gather_parts(halves, parts):
    if parts != 4 or len(halves) != 2:
        return [halves] + [[swap(h, "rep", i) for h in halves] for i in range(1, parts)]
    one = [swap(h, "rep", 1) for h in halves]
    two = [swap(h, "rep", 2) for h in halves]
    three = [swap(two[0], "rep", 1), swap(one[1], "rep", 2)]
    return [halves, one, two, three]


def shards(chunks, query, key_proj, value, poles, residues, skip, w_out):
    tokens, channels = query.shape
    width = w_out.shape[1]
    members = lax.axis_size("seq")
    parts = lax.axis_size("rep")
    order = poles.shape[1]
    tiles = channels // LANES
    part_width = width // parts
    columns = part_width // chunks
    remote = pltpu.HBM

    sliced = call(
        slice_kernel,
        [((w_out.shape[0], columns), BF16)] * chunks,
        (w_out,),
        [pltpu.SemaphoreType.DMA((chunks,))],
        inputs=[remote],
    )
    weights = []
    for n in range(chunks):
        rows, places = gather_rows(sliced[n], members)
        weights.append(rows)

    poles = poles.T
    residues = residues.T
    skip = skip.reshape(tiles, LANES)
    sums = ((tiles * tokens, LANES), F32)
    modes = pltpu.VMEM((tiles * order, LANES), F32)
    work = tokens * channels * order
    kept, sent, rate = call(
        state_kernel,
        [((order, tiles // 2, LANES), F32)] * 3,
        (key_proj, value, poles),
        [
            pltpu.VMEM((tokens, channels), BF16),
            pltpu.VMEM((tokens, channels), BF16),
            pltpu.VMEM((order, channels), F32),
            pltpu.VMEM(*sums),
            modes,
            pltpu.SemaphoreType.DMA((3,)),
        ],
        flops=2 * work,
        inputs=[remote] * 3,
    )
    own, arrived, rest, rest_arrived, span = carry_in(kept, sent, rate, members)
    (local,) = call(
        local_kernel,
        [sums],
        (key_proj, value, poles, residues, skip),
        [modes, modes, pltpu.VMEM((order, SUBLANES, LANES), F32)],
        flops=4 * work,
    )
    halves = call(
        functools.partial(carry_kernel, span),
        [((tokens // 2, channels), BF16)] * 2,
        (query, local, poles, residues, own, arrived, rest, rest_arrived),
        [
            pltpu.VMEM(*sums),
            pltpu.VMEM((tokens // 16, order, SUBLANES, LANES), F32),
            modes,
            modes,
            pltpu.VMEM((tokens, channels), BF16),
            pltpu.SemaphoreType.DMA,
        ],
        flops=2 * work,
        inputs=[remote] + [pltpu.VMEM] * 7,
    )
    gathered = gather_parts(list(halves), parts)

    def project(group, first, last, earlier=None, final=True):
        held = sum(group, [])
        rows = sum(h.shape[0] for h in held)
        chosen = sum((w[first:last] for w in weights), [])
        shapes = [((tokens, part_width), BF16)] * len(group) if final else [((rows, columns), F32)] * chunks
        return call(
            functools.partial(
                project_kernel, len(held), lambda seq: places(seq)[first:last], chunks, earlier is not None
            ),
            shapes,
            (*held, *chosen, *(earlier or ())),
            flops=2 * rows * chosen[0].shape[0] * len(chosen) * columns,
        )

    count = len(weights[0])
    split = max(count - 2, 0)
    if split > 0:
        partial = project(gathered[:-1], 0, split, final=False)
        blocks = project(gathered[:-1], split, count, earlier=partial)
    else:
        blocks = project(gathered[:-1], 0, count)
    blocks = list(blocks) + list(project(gathered[-1:], 0, count))
    pieces = [blocks[0]] + [swap(blocks[i], "rep", i) for i in range(1, parts)]
    mixed = None
    for group in (range(parts // 2), range(parts // 2, parts)):
        first = mixed is None
        (mixed,) = call(
            functools.partial(place_kernel, group, not first),
            [((tokens, width), BF16)],
            ([] if first else [mixed]) + [pieces[i] for i in group],
            [pltpu.SemaphoreType.DMA((len(group),))],
            inputs=([] if first else [remote]) + [pltpu.VMEM] * len(group),
            outputs=remote,
            aliases=None if first else {0: 0},
        )
    return mixed


def solution(mesh):
    chunks = 2

    def body(*args):
        return shards(chunks, *args)

    return jax.shard_map(
        body,
        mesh=mesh,
        in_specs=(
            P(("rep", "seq"), None),
            P(("rep", "seq"), None),
            P(("rep", "seq"), None),
            P(),
            P(),
            P(),
            P("seq", None),
        ),
        out_specs=P(("rep", "seq"), None),
        check_vma=False,
    )
```
